768 devices in a mesh: row: 16 (over y_hi, x, core), col: 48 (over z, y_lo).
Axes of the slice: x: 4, y: 8 (y_hi: 2, y_lo: 4; y = y_hi * 4 + y_lo), z: 12, core: 2. Of those that a mesh axis runs over, the one named last changes fastest.
Arguments:
- object_tiles: float32 [2, 2, 2048, 6144], P(None, None, 'row', 'col'), may hold values from -3 to 3
- positions: int32 [16, 48, 6, 2], P('row', 'col'), may hold values from 0 to 128, as said below
- probe: float32 [2, 128, 128], replicated, may hold values from -4.2 to 4.2
- phase: float32 [128, 128], replicated, may hold values from -3.140625 to 3.140625
- intensity: float32 [16, 48, 6, 128, 128], P('row', 'col'), may hold values from 0.05 to 1
Outputs:
- updated_tiles: float32 [2, 2, 4096, 12288], P(None, None, 'row', 'col')
The draws below stay inside these ranges and needn't reach their ends.
Inputs may be any that keep to these rules, and one draw needn't show every extreme that they name: `positions`: every window of 128 x 128 pixels lies inside the object. In every tile probe 0 takes the least and probe 1 the greatest row offset that this allows, probe 2 the least and probe 3 the greatest column offset.
All inputs are finite; a program needn't handle non-finite values.
Results may differ from the reference program's by a relative error of at most 0.0003.
Values sent between devices are 32-bit elements; how exact they have to be, the bound alone decides.
No kernel may reach another device: no remote copies, remote signals or barrier semaphores. Data moves between devices by JAX's collectives and lax.ppermute only.
A program may use at most 32 MiB of HBM per device.

```python
import math
import jax
import jax.numpy as jnp
from jax import lax

PROBE = 128
PROBES = 6
MARGIN = 64
TILE = 128
PADW = 256
TROWS = 16
TCOLS = 48


def draw_positions(key, part):
    reach_max = PADW - PROBE
    tile_row = jnp.arange(TROWS, dtype=jnp.int32)[:, None, None]
    tile_col = jnp.arange(TCOLS, dtype=jnp.int32)[None, :, None]
    number = jnp.arange(PROBES, dtype=jnp.int32)[None, None, :]
    low_row = jnp.where(tile_row == 0, MARGIN, 0)
    high_row = jnp.where(tile_row == TROWS - 1, reach_max - MARGIN, reach_max)
    low_col = jnp.where(tile_col == 0, MARGIN, 0)
    high_col = jnp.where(tile_col == TCOLS - 1, reach_max - MARGIN, reach_max)
    raw_bits = jax.random.randint(key, (TROWS, TCOLS, PROBES, 2), 0, 1 << 20, dtype=jnp.int32)
    row_offsets = low_row + raw_bits[..., 0] % (high_row - low_row + 1)
    row_offsets = jnp.where(number == 0, low_row, jnp.where(number == 1, high_row, row_offsets))
    col_offsets = low_col + raw_bits[..., 1] % (high_col - low_col + 1)
    col_offsets = jnp.where(number == 2, low_col, jnp.where(number == 3, high_col, col_offsets))
    return jnp.stack([row_offsets, col_offsets], -1).astype(jnp.int32)


def shard_levels(own_key, extent, split, low, largest):
    factor_of, own = 1.0, jax.random.fold_in(own_key, 6)
    for position, blocks in split:
        heights = jnp.exp(jax.random.uniform(jax.random.fold_in(own, position), (blocks,), jnp.float32, low / len(split), largest / len(split)))
        factor_of = factor_of * jnp.repeat(heights, extent[position] // blocks).reshape([-1 if axis == position else 1 for axis in range(len(extent))])
    return factor_of


def bell_draw(stream_key, dims, spread, bound, split=(), kind=jnp.bfloat16):
    entries = spread * jax.random.normal(stream_key, dims, jnp.float32)
    if split:
        entries = entries * shard_levels(stream_key, dims, split, -0.22, 0.18)
    return jnp.clip(entries, -bound, bound).astype(kind)


def setup_inputs(seed: int = 0) -> dict:
    keys = jax.random.split(jax.random.key(seed), 6)
    object_tiles = bell_draw(keys[0], (2, 2, TROWS * TILE, TCOLS * TILE), 0.5, 3.0, ((2, 16), (3, 48)), jnp.float32)
    positions = draw_positions(jax.random.fold_in(keys[5], 71), 0)
    probe = bell_draw(keys[2], (2, PROBE, PROBE), 0.7, 4.2, (), jnp.float32)
    phase = jnp.clip(jax.random.uniform(keys[3], (PROBE, PROBE), jnp.float32, -3.140625, 3.140625), -3.140625, 3.140625)
    intensity = jnp.clip(jnp.exp(math.log(1.0) - 2.9957323 * jax.random.uniform(keys[4], (TROWS, TCOLS, PROBES, PROBE, PROBE), jnp.float32) ** shard_levels(keys[4], (TROWS, TCOLS, PROBES, PROBE, PROBE), ((0, 16), (1, 48)), -0.2, 0.2)), 0.05, 1.0)
    return {"object_tiles": object_tiles, "positions": positions, "probe": probe, "phase": phase, "intensity": intensity}


step_size = 2.0


def wave_gradients(first, second, probe_wave, propagator, measured):
    entry = probe_wave * first
    inner = jnp.fft.ifft2(propagator * jnp.fft.fft2(entry, norm="ortho"), norm="ortho")
    leaving = inner * second
    far = jnp.fft.fft2(leaving, norm="ortho")
    misfit = jnp.real(far) ** 2 + jnp.imag(far) ** 2 - measured
    back = jnp.fft.ifft2(misfit * far, norm="ortho")
    grad_second = jnp.conj(inner) * back
    wave = jnp.conj(second) * back
    wave = jnp.fft.ifft2(jnp.conj(propagator) * jnp.fft.fft2(wave, norm="ortho"), norm="ortho")
    grad_first = jnp.conj(probe_wave) * wave
    return jnp.stack([jnp.stack([jnp.real(grad_first), jnp.imag(grad_first)]), jnp.stack([jnp.real(grad_second), jnp.imag(grad_second)])])


def reference(object_tiles, positions, probe, phase, intensity):
    whole = jnp.pad(object_tiles, ((0, 0), (0, 0), (MARGIN, MARGIN), (MARGIN, MARGIN)))
    probe_wave = lax.complex(probe[0], probe[1])
    propagator = lax.complex(jnp.cos(phase), jnp.sin(phase))
    flat_positions = positions.reshape(TROWS * TCOLS, PROBES, 2)
    flat_intensity = intensity.reshape(TROWS * TCOLS, PROBES, PROBE, PROBE)
    anchor = jnp.zeros((), jnp.int32)

    def one_tile(gradient, tile_number):
        tile_row = (tile_number // TCOLS).astype(jnp.int32)
        tile_col = (tile_number % TCOLS).astype(jnp.int32)
        offsets = flat_positions[tile_number]
        measured = flat_intensity[tile_number]
        for number in range(PROBES):
            top = (tile_row * TILE + offsets[number, 0]).astype(jnp.int32)
            left = (tile_col * TILE + offsets[number, 1]).astype(jnp.int32)
            corner = (anchor, anchor, top, left)
            window = lax.dynamic_slice(whole, corner, (2, 2, PROBE, PROBE))
            first = lax.complex(window[0, 0], window[0, 1])
            second = lax.complex(window[1, 0], window[1, 1])
            grads = wave_gradients(first, second, probe_wave, propagator, measured[number])
            block = lax.dynamic_slice(gradient, corner, (2, 2, PROBE, PROBE)) + grads
            gradient = lax.dynamic_update_slice(gradient, block, corner)
        return gradient, None

    gradient, unused = lax.scan(one_tile, jnp.zeros_like(whole), jnp.arange(TROWS * TCOLS, dtype=jnp.int32))
    updated = whole - step_size * gradient
    row_index = (jnp.arange(TROWS, dtype=jnp.int32)[:, None] * TILE + jnp.arange(PADW, dtype=jnp.int32)[None, :]).reshape(-1)
    col_index = (jnp.arange(TCOLS, dtype=jnp.int32)[:, None] * TILE + jnp.arange(PADW, dtype=jnp.int32)[None, :]).reshape(-1)
    return jnp.take(jnp.take(updated, row_index, axis=2), col_index, axis=3)
```

```python
import jax
import jax.numpy as jnp
import numpy as np
from jax import lax
from jax.experimental import pallas as pl
from jax.experimental.pallas import tpu as pltpu
from jax.sharding import PartitionSpec as P

N = 128
HALF = 64
WIDE = 256
STEP = 2.0
BF = jnp.bfloat16
F32 = jnp.float32


def tables():
    counter = np.arange(N)
    angles = 2.0 * np.pi / N * (counter[:, None] * counter[None, :] % N)
    cos, sin = np.cos(angles), np.sin(angles)
    first = np.block([[cos, -sin], [sin, cos]]) / N
    second = np.block([[cos, sin], [-sin, cos]])
    out = []
    for table in (first, second):
        table = table.astype(np.float32)
        high = table.astype(BF)
        low = (table - high.astype(np.float32)).astype(BF)
        out += [high, low]
    return np.stack(out)


def split(value):
    high = value.astype(BF)
    return high, (value - high.astype(F32)).astype(BF)


def times(ar, ai, br, bi):
    return ar * br - ai * bi, ar * bi + ai * br


def times_conj(ar, ai, br, bi):
    return ar * br + ai * bi, ar * bi - ai * br


def pack_kernel(obj, to_left, to_right):
    lane = lax.broadcasted_iota(jnp.int32, (N, N), 1)
    for s in range(2):
        re, im = obj[s, 0], obj[s, 1]
        to_left[s] = jnp.where(lane < HALF, re, pltpu.roll(im, HALF, 1))
        to_right[s] = jnp.where(lane < HALF, pltpu.roll(re, HALF, 1), im)


def extend_kernel(obj, from_left, from_right, top, bottom):
    lane = lax.broadcasted_iota(jnp.int32, (N, N), 1)
    for s in range(2):
        left, right = from_left[s], from_right[s]
        re = jnp.where(lane < HALF, right, pltpu.roll(left, HALF, 1))
        im = jnp.where(lane < HALF, pltpu.roll(right, HALF, 1), left)
        for q, side in enumerate((re, im)):
            centre = obj[s, q]
            top[s, q, :, :N] = centre[:HALF]
            bottom[s, q, :, :N] = centre[HALF:]
            top[s, q, :, N:] = side[:HALF]
            bottom[s, q, :, N:] = side[HALF:]


def main_kernel(pos, up, top, bottom, down, probe, phase, inten, tabs, g_up, g_mid, g_down,
                pad, acc, hre, him, xh, xl, zh, zl, inner, second):
    for k, ref in enumerate((up, top, bottom, down)):
        for t in range(2):
            pad[:, :, t, k * HALF:(k + 1) * HALF, :] = ref[:, :, :, t * N:(t + 1) * N]
    acc[...] = jnp.zeros_like(acc)
    hre[...] = jnp.cos(phase[...])
    him[...] = jnp.sin(phase[...])

    lane = lax.broadcasted_iota(jnp.int32, (N, N), 1)

    def window(s, q, k):
        rows = pl.ds(pos[k, 0], N)
        begin = lax.rem(pos[k, 1] + 3 * HALF, WIDE)
        tile = begin // N
        turn = lax.rem(WIDE - begin, N)
        one = pltpu.roll(pad[s, q, tile, rows, :], turn, 1)
        two = pltpu.roll(pad[s, q, 1 - tile, rows, :], turn, 1)
        return jnp.where(lane < N - lax.rem(begin, N), one, two)

    def scatter(s, q, k, value):
        rows = pl.ds(pos[k, 0], N)
        moved = pltpu.roll(value, lax.rem(pos[k, 1], N), 1)
        fits = lane >= pos[k, 1]
        acc[s, q, 0, rows, :] = acc[s, q, 0, rows, :] + jnp.where(fits, moved, 0.0)
        acc[s, q, 1, rows, :] = acc[s, q, 1, rows, :] + jnp.where(fits, 0.0, moved)

    def put(g, b, re, im):
        rows = slice(b * N, (b + 1) * N)
        for q, part in enumerate((re, im)):
            high, low = split(part)
            xh[g, rows, q * N:(q + 1) * N] = high
            xl[g, rows, q * N:(q + 1) * N] = low

    def dot(a, b):
        return jnp.dot(a, b, preferred_element_type=F32)

    def right(g, t):
        high, low = xh[g], xl[g]
        y = dot(high, tabs[2 * t]) + dot(low, tabs[2 * t]) + dot(high, tabs[2 * t + 1])
        for b in range(2):
            for q in range(2):
                h, l = split(y[b * N:(b + 1) * N, q * N:(q + 1) * N])
                zh[g, q * N:(q + 1) * N, b * N:(b + 1) * N] = h
                zl[g, q * N:(q + 1) * N, b * N:(b + 1) * N] = l

    def left(g, t):
        high, low = zh[g], zl[g]
        y = dot(tabs[2 * t], high) + dot(tabs[2 * t], low) + dot(tabs[2 * t + 1], high)
        return [(y[:N, b * N:(b + 1) * N], y[N:, b * N:(b + 1) * N]) for b in range(2)]

    groups = range(3)
    for g in groups:
        for b in range(2):
            k = 2 * g + b
            re, im = times(probe[0], probe[1], window(0, 0, k), window(0, 1, k))
            put(g, b, re, im)
    for g in groups:
        right(g, 0)
    for g in groups:
        for b, (re, im) in enumerate(left(g, 1)):
            put(g, b, *times(hre[...], him[...], re, im))
    for g in groups:
        right(g, 1)
    for g in groups:
        for b, (re, im) in enumerate(left(g, 0)):
            k = 2 * g + b
            inner[k, 0], inner[k, 1] = re, im
            o_re, o_im = window(1, 0, k), window(1, 1, k)
            second[k, 0], second[k, 1] = o_re, o_im
            put(g, b, *times(re, im, o_re, o_im))
    for g in groups:
        right(g, 0)
    for g in groups:
        for b, (re, im) in enumerate(left(g, 1)):
            misfit = re * re + im * im - inten[2 * g + b]
            put(g, b, misfit * re, misfit * im)
    for g in groups:
        right(g, 1)
    for g in groups:
        for b, (re, im) in enumerate(left(g, 0)):
            k = 2 * g + b
            put(g, b, *times_conj(second[k, 0], second[k, 1], re, im))
            for q, part in enumerate(times_conj(inner[k, 0], inner[k, 1], re, im)):
                scatter(1, q, k, part)
    for g in groups:
        right(g, 0)
    for g in groups:
        for b, (re, im) in enumerate(left(g, 1)):
            put(g, b, *times_conj(hre[...], him[...], re, im))
    for g in groups:
        right(g, 1)
    for g in groups:
        for b, (re, im) in enumerate(left(g, 0)):
            k = 2 * g + b
            for q, part in enumerate(times_conj(probe[0], probe[1], re, im)):
                scatter(0, q, k, part)
    for t in range(2):
        cols = slice(t * N, (t + 1) * N)
        g_up[..., cols] = acc[:, :, t, :HALF, :]
        g_mid[..., cols] = acc[:, :, t, HALF:3 * HALF, :]
        g_down[..., cols] = acc[:, :, t, 3 * HALF:, :]


def fold_kernel(mid, from_up, from_down, left_half, right_half):
    for k, ref in enumerate((from_up, from_down)):
        rows = slice(k * HALF, (k + 1) * HALF)
        total = mid[:, :, rows, :] + ref[...]
        left_half[:, :, rows, :] = total[..., :N]
        right_half[:, :, rows, :] = total[..., N:]


def update_kernel(top, bottom, left_half, right_half, from_left, from_right, out_top, out_bottom):
    for k, (ref, out) in enumerate(((top, out_top), (bottom, out_bottom))):
        rows = slice(k * HALF, (k + 1) * HALF)
        for s in range(2):
            for q in range(2):
                values = pltpu.roll(ref[s, q], HALF, 1)
                out[s, q, :, :N] = values[:, :N] - STEP * (left_half[s, q, rows] + from_left[s, q, rows])
                out[s, q, :, N:] = values[:, N:] - STEP * (right_half[s, q, rows] + from_right[s, q, rows])


VM = pl.BlockSpec(memory_space=pltpu.VMEM)
SM = pl.BlockSpec(memory_space=pltpu.SMEM)


def shape(*dims):
    return jax.ShapeDtypeStruct(dims, F32)


def call(kernel, outs, args, scratch=(), smem=0, limit=None):
    return pl.pallas_call(
        kernel,
        out_shape=outs,
        in_specs=[SM] * smem + [VM] * (len(args) - smem),
        out_specs=[VM] * len(outs),
        scratch_shapes=list(scratch),
        compiler_params=pltpu.CompilerParams(vmem_limit_bytes=limit),
    )(*args)


def shift(value, axis, step):
    count = lax.axis_size(axis)
    pairs = [(i, i + step) for i in range(count) if 0 <= i + step < count]
    return lax.ppermute(value, axis, pairs)


def per_device(obj, positions, probe, phase, intensity):
    to_left, to_right = call(pack_kernel, [shape(2, N, N)] * 2, [obj])
    from_left = shift(to_right, "col", 1)
    from_right = shift(to_left, "col", -1)
    strip = shape(2, 2, HALF, WIDE)
    top, bottom = call(extend_kernel, [strip] * 2, [obj, from_left, from_right])
    up = shift(bottom, "row", 1)
    down = shift(top, "row", -1)
    scratch = [
        pltpu.VMEM((2, 2, 2, WIDE, N), F32), pltpu.VMEM((2, 2, 2, WIDE, N), F32),
        pltpu.VMEM((N, N), F32), pltpu.VMEM((N, N), F32),
        pltpu.VMEM((3, WIDE, WIDE), BF), pltpu.VMEM((3, WIDE, WIDE), BF),
        pltpu.VMEM((3, WIDE, WIDE), BF), pltpu.VMEM((3, WIDE, WIDE), BF),
        pltpu.VMEM((6, 2, N, N), F32), pltpu.VMEM((6, 2, N, N), F32),
    ]
    g_up, g_mid, g_down = call(
        main_kernel, [strip, shape(2, 2, N, WIDE), strip],
        [positions[0, 0], up, top, bottom, down, probe, phase, intensity[0, 0], jnp.asarray(tables())],
        scratch, smem=1, limit=40 << 20)
    g_from_down = shift(g_up, "row", -1)
    g_from_up = shift(g_down, "row", 1)
    half = shape(2, 2, N, N)
    left_half, right_half = call(fold_kernel, [half] * 2, [g_mid, g_from_up, g_from_down])
    h_from_left = shift(right_half, "col", 1)
    h_from_right = shift(left_half, "col", -1)
    out_top, out_bottom = call(
        update_kernel, [strip] * 2, [top, bottom, left_half, right_half, h_from_left, h_from_right])
    above = shift(out_bottom, "row", 1)
    below = shift(out_top, "row", -1)
    return jnp.concatenate([above, out_top, out_bottom, below], axis=2)


def solution(mesh):
    return jax.shard_map(
        per_device,
        mesh=mesh,
        in_specs=(
            P(None, None, "row", "col"),
            P("row", "col", None, None),
            P(),
            P(),
            P("row", "col", None, None, None),
        ),
        out_specs=P(None, None, "row", "col"),
        check_vma=False,
    )
```

```python
import functools

import jax
import jax.numpy as jnp
import numpy as np
from jax import lax
from jax.experimental import pallas as pl
from jax.experimental.pallas import tpu as pltpu
from jax.sharding import PartitionSpec as P

N = 128
HALF = 64
WIDE = 256
STEP = 2.0
BF = jnp.bfloat16
F32 = jnp.float32


def tables():
    counter = np.arange(N)
    angles = 2.0 * np.pi / N * (counter[:, None] * counter[None, :] % N)
    cos, sin = np.cos(angles), np.sin(angles)
    first = np.block([[cos, -sin], [sin, cos]]) / N
    second = np.block([[cos, sin], [-sin, cos]])
    out = []
    for table in (first, second):
        table = table.astype(np.float32)
        high = table.astype(BF)
        low = (table - high.astype(np.float32)).astype(BF)
        out += [high, low]
    return np.stack(out)


def split(value):
    high = value.astype(BF)
    return high, (value - high.astype(F32)).astype(BF)


def times(ar, ai, br, bi):
    return ar * br - ai * bi, ar * bi + ai * br


def times_conj(ar, ai, br, bi):
    return ar * br + ai * bi, ar * bi - ai * br


def parity_of(axis):
    return lax.rem(lax.axis_index(axis), 2)


def choose(flag, one, two):
    return jnp.where(flag, one, two)


def pack_kernel(obj, send_a, send_b):
    even = parity_of("col") == 0
    lane = lax.broadcasted_iota(jnp.int32, (N, N), 1)
    for s in range(2):
        re, im = obj[s, 0], obj[s, 1]
        to_left = jnp.where(lane < HALF, re, pltpu.roll(im, HALF, 1))
        to_right = jnp.where(lane < HALF, pltpu.roll(re, HALF, 1), im)
        send_a[s] = choose(even, to_right, to_left)
        send_b[s] = choose(even, to_left, to_right)


def extend_kernel(obj, got_a, got_b, send_a, send_b):
    even_row, even = parity_of("row") == 0, parity_of("col") == 0
    lane = lax.broadcasted_iota(jnp.int32, (N, N), 1)
    for s in range(2):
        left, right = choose(even, got_b[s], got_a[s]), choose(even, got_a[s], got_b[s])
        re = jnp.where(lane < HALF, right, pltpu.roll(left, HALF, 1))
        im = jnp.where(lane < HALF, pltpu.roll(right, HALF, 1), left)
        for q, side in enumerate((re, im)):
            for t, part in enumerate((obj[s, q], side)):
                cols = slice(t * N, (t + 1) * N)
                send_a[s, q, :, cols] = choose(even_row, part[HALF:], part[:HALF])
                send_b[s, q, :, cols] = choose(even_row, part[:HALF], part[HALF:])


def main_kernel(pos, own_a, own_b, got_a, got_b, probe, phase, inten, tabs, send_a, g_mid, send_b,
                measured, sem, pad, acc, hre, him, xh, xl, zh, zl, inner, second):
    parity = parity_of("row")
    starts = (2 - parity, 1 + parity, 3 - 3 * parity, 3 * parity)
    for start, ref in zip(starts, (own_a, own_b, got_a, got_b)):
        rows = pl.ds(pl.multiple_of(start * HALF, HALF), HALF)
        for t in range(2):
            pad[:, :, t, rows, :] = ref[:, :, :, t * N:(t + 1) * N]
    fetch = pltpu.make_async_copy(inten.at[0, 0], measured, sem)
    fetch.start()
    acc[...] = jnp.zeros_like(acc)
    hre[...] = jnp.cos(phase[...])
    him[...] = jnp.sin(phase[...])

    lane = lax.broadcasted_iota(jnp.int32, (N, N), 1)

    def window(s, q, k):
        rows = pl.ds(pos[k, 0], N)
        begin = lax.rem(pos[k, 1] + 3 * HALF, WIDE)
        tile = begin // N
        turn = lax.rem(WIDE - begin, N)
        one = pltpu.roll(pad[s, q, tile, rows, :], turn, 1)
        two = pltpu.roll(pad[s, q, 1 - tile, rows, :], turn, 1)
        return jnp.where(lane < N - lax.rem(begin, N), one, two)

    def scatter(s, q, k, value):
        rows = pl.ds(pos[k, 0], N)
        moved = pltpu.roll(value, lax.rem(pos[k, 1], N), 1)
        fits = lane >= pos[k, 1]
        acc[s, q, 0, rows, :] = acc[s, q, 0, rows, :] + jnp.where(fits, moved, 0.0)
        acc[s, q, 1, rows, :] = acc[s, q, 1, rows, :] + jnp.where(fits, 0.0, moved)

    def put(g, b, re, im):
        rows = slice(b * N, (b + 1) * N)
        for q, part in enumerate((re, im)):
            high, low = split(part)
            xh[g, rows, q * N:(q + 1) * N] = high
            xl[g, rows, q * N:(q + 1) * N] = low

    def dot(a, b):
        return jnp.dot(a, b, preferred_element_type=F32)

    def right(g, t):
        high, low = xh[g], xl[g]
        y = dot(high, tabs[2 * t]) + dot(low, tabs[2 * t]) + dot(high, tabs[2 * t + 1])
        for b in range(2):
            for q in range(2):
                h, l = split(y[b * N:(b + 1) * N, q * N:(q + 1) * N])
                zh[g, q * N:(q + 1) * N, b * N:(b + 1) * N] = h
                zl[g, q * N:(q + 1) * N, b * N:(b + 1) * N] = l

    def left(g, t):
        high, low = zh[g], zl[g]
        y = dot(tabs[2 * t], high) + dot(tabs[2 * t], low) + dot(tabs[2 * t + 1], high)
        return [(y[:N, b * N:(b + 1) * N], y[N:, b * N:(b + 1) * N]) for b in range(2)]

    groups = range(3)
    for g in groups:
        for b in range(2):
            k = 2 * g + b
            re, im = times(probe[0], probe[1], window(0, 0, k), window(0, 1, k))
            put(g, b, re, im)
    for g in groups:
        right(g, 0)
    for g in groups:
        for b, (re, im) in enumerate(left(g, 1)):
            put(g, b, *times(hre[...], him[...], re, im))
    for g in groups:
        right(g, 1)
    for g in groups:
        for b, (re, im) in enumerate(left(g, 0)):
            k = 2 * g + b
            inner[k, 0], inner[k, 1] = re, im
            o_re, o_im = window(1, 0, k), window(1, 1, k)
            second[k, 0], second[k, 1] = o_re, o_im
            put(g, b, *times(re, im, o_re, o_im))
    for g in groups:
        right(g, 0)
    fetch.wait()
    for g in groups:
        for b, (re, im) in enumerate(left(g, 1)):
            misfit = re * re + im * im - measured[2 * g + b]
            put(g, b, misfit * re, misfit * im)
    for g in groups:
        right(g, 1)
    for g in groups:
        for b, (re, im) in enumerate(left(g, 0)):
            k = 2 * g + b
            put(g, b, *times_conj(second[k, 0], second[k, 1], re, im))
            for q, part in enumerate(times_conj(inner[k, 0], inner[k, 1], re, im)):
                scatter(1, q, k, part)
    for g in groups:
        right(g, 0)
    for g in groups:
        for b, (re, im) in enumerate(left(g, 1)):
            put(g, b, *times_conj(hre[...], him[...], re, im))
    for g in groups:
        right(g, 1)
    for g in groups:
        for b, (re, im) in enumerate(left(g, 0)):
            k = 2 * g + b
            for q, part in enumerate(times_conj(probe[0], probe[1], re, im)):
                scatter(0, q, k, part)
    for t in range(2):
        cols = slice(t * N, (t + 1) * N)
        g_mid[..., cols] = acc[:, :, t, HALF:3 * HALF, :]
        for start, ref in zip(starts[2:], (send_a, send_b)):
            rows = pl.ds(pl.multiple_of(start * HALF, HALF), HALF)
            ref[..., cols] = acc[:, :, t, rows, :]


def fold_kernel(mid, got_a, got_b, send_a, send_b):
    even_row, even = parity_of("row") == 0, parity_of("col") == 0
    above, below = choose(even_row, got_b[...], got_a[...]), choose(even_row, got_a[...], got_b[...])
    for k, ref in enumerate((above, below)):
        rows = slice(k * HALF, (k + 1) * HALF)
        total = mid[:, :, rows, :] + ref
        send_a[:, :, rows, :] = choose(even, total[..., N:], total[..., :N])
        send_b[:, :, rows, :] = choose(even, total[..., :N], total[..., N:])


def update_kernel(own_a, own_b, sent_a, sent_b, got_a, got_b, send_a, send_b):
    even_row, even = parity_of("row") == 0, parity_of("col") == 0
    for s in range(2):
        for q in range(2):
            one, two = sent_a[s, q] + got_a[s, q], sent_b[s, q] + got_b[s, q]
            total = [choose(even, two, one), choose(even, one, two)]
            first, last = own_a[s, q], own_b[s, q]
            top, bottom = choose(even_row, last, first), choose(even_row, first, last)
            out = []
            for k, ref in enumerate((top, bottom)):
                values = pltpu.roll(ref, HALF, 1)
                rows = slice(k * HALF, (k + 1) * HALF)
                out.append([values[:, t * N:(t + 1) * N] - STEP * total[t][rows] for t in range(2)])
            for t in range(2):
                cols = slice(t * N, (t + 1) * N)
                send_a[s, q, :, cols] = choose(even_row, out[1][t], out[0][t])
                send_b[s, q, :, cols] = choose(even_row, out[0][t], out[1][t])


HBM = pl.BlockSpec(memory_space=pltpu.HBM)
VM = pl.BlockSpec(memory_space=pltpu.VMEM)
SM = pl.BlockSpec(memory_space=pltpu.SMEM)


def shape(*dims):
    return jax.ShapeDtypeStruct(dims, F32)


def call(kernel, outs, args, scratch=(), smem=0, limit=6, anys=(), cost=1 << 20):
    specs = [SM] * smem + [VM] * (len(args) - smem)
    for k in anys:
        specs[k] = HBM
    return pl.pallas_call(
        kernel,
        out_shape=outs,
        in_specs=specs,
        out_specs=[VM] * len(outs),
        scratch_shapes=list(scratch),
        cost_estimate=pl.CostEstimate(flops=cost, bytes_accessed=cost, transcendentals=0),
        compiler_params=pltpu.CompilerParams(vmem_limit_bytes=limit << 20),
    )(*args)


def place_kernel(starts, *refs):
    value_a, value_b, out, sems = refs[0], refs[1], refs[-2], refs[-1]
    parity = parity_of("row")
    copies = []
    for k, (value, (even, odd)) in enumerate(zip((value_a, value_b), starts)):
        rows = pl.ds(pl.multiple_of((even + (odd - even) * parity) * HALF, HALF), HALF)
        copies.append(pltpu.make_async_copy(value, out.at[:, :, rows, :], sems.at[k]))
    for copy in copies:
        copy.start()
    for copy in copies:
        copy.wait()


def put_rows(value_a, value_b, starts, out=None):
    args = [value_a, value_b] + ([] if out is None else [out])
    return pl.pallas_call(
        functools.partial(place_kernel, starts),
        out_shape=shape(2, 2, WIDE, WIDE),
        in_specs=[VM, VM] + [HBM] * (len(args) - 2),
        out_specs=HBM,
        scratch_shapes=[pltpu.SemaphoreType.DMA((2,))],
        input_output_aliases={} if out is None else {2: 0},
        cost_estimate=pl.CostEstimate(flops=1 << 20, bytes_accessed=1 << 20, transcendentals=0),
        compiler_params=pltpu.CompilerParams(vmem_limit_bytes=2 << 20),
    )(*args)


def swap(value_a, value_b, axis):
    count = lax.axis_size(axis)

    def pairs(first):
        found = [(i, i + 1) for i in range(first, count - 1, 2)]
        return found + [(target, source) for source, target in found]

    got_b = lax.ppermute(value_b, axis, pairs(1))
    got_a = lax.ppermute(value_a, axis, pairs(0))
    return got_a, got_b


def per_device(obj, positions, probe, phase, intensity):
    strip, half = shape(2, 2, HALF, WIDE), shape(2, 2, N, N)
    side_a, side_b = call(pack_kernel, [shape(2, N, N)] * 2, [obj])
    side_a, side_b = swap(side_a, side_b, "col")
    own_a, own_b = call(extend_kernel, [strip] * 2, [obj, side_a, side_b])
    far_a, far_b = swap(own_a, own_b, "row")
    scratch = [
        pltpu.VMEM((6, N, N), F32), pltpu.SemaphoreType.DMA,
        pltpu.VMEM((2, 2, 2, WIDE, N), F32), pltpu.VMEM((2, 2, 2, WIDE, N), F32),
        pltpu.VMEM((N, N), F32), pltpu.VMEM((N, N), F32),
        pltpu.VMEM((3, WIDE, WIDE), BF), pltpu.VMEM((3, WIDE, WIDE), BF),
        pltpu.VMEM((3, WIDE, WIDE), BF), pltpu.VMEM((3, WIDE, WIDE), BF),
        pltpu.VMEM((6, 2, N, N), F32), pltpu.VMEM((6, 2, N, N), F32),
    ]
    g_a, g_mid, g_b = call(
        main_kernel, [strip, shape(2, 2, N, WIDE), strip],
        [positions[0, 0], own_a, own_b, far_a, far_b, probe, phase,
         pltpu.with_memory_space_constraint(intensity, pltpu.HBM), jnp.asarray(tables())],
        scratch, smem=1, limit=24, anys=(7,))
    g_a, g_b = swap(g_a, g_b, "row")
    half_a, half_b = call(fold_kernel, [half] * 2, [g_mid, g_a, g_b])
    h_a, h_b = swap(half_a, half_b, "col")
    new_a, new_b = call(update_kernel, [strip] * 2, [own_a, own_b, half_a, half_b, h_a, h_b])
    out_a, out_b = swap(new_a, new_b, "row")
    out = put_rows(new_a, new_b, ((2, 1), (1, 2)))
    return put_rows(out_a, out_b, ((3, 0), (0, 3)), out)


def solution(mesh):
    return jax.shard_map(
        per_device,
        mesh=mesh,
        in_specs=(
            P(None, None, "row", "col"),
            P("row", "col", None, None),
            P(),
            P(),
            P("row", "col", None, None, None),
        ),
        out_specs=P(None, None, "row", "col"),
        check_vma=False,
    )
```

```python
import functools

import jax
import jax.numpy as jnp
import numpy as np
from jax import lax
from jax.experimental import pallas as pl
from jax.experimental.pallas import tpu as pltpu
from jax.sharding import PartitionSpec as P

N = 128
HALF = 64
WIDE = 256
STEP = 2.0
BF = jnp.bfloat16
F32 = jnp.float32


def tables():
    counter = np.arange(N)
    angles = 2.0 * np.pi / N * (counter[:, None] * counter[None, :] % N)
    cos, sin = np.cos(angles), np.sin(angles)
    first = np.block([[cos, -sin], [sin, cos]]) / N
    second = np.block([[cos, sin], [-sin, cos]])
    out = []
    for table in (first, second):
        table = table.astype(np.float32)
        high = table.astype(BF)
        low = (table - high.astype(np.float32)).astype(BF)
        out += [high, low]
    return np.stack(out)


def split(value):
    high = value.astype(BF)
    return high, (value - high.astype(F32)).astype(BF)


def times(ar, ai, br, bi):
    return ar * br - ai * bi, ar * bi + ai * br


def times_conj(ar, ai, br, bi):
    return ar * br + ai * bi, ar * bi - ai * br


def parity_of(axis):
    return lax.rem(lax.axis_index(axis), 2)


def choose(flag, one, two):
    return jnp.where(flag, one, two)


def pack_kernel(obj, send_a, send_b):
    even = parity_of("col") == 0
    lane = lax.broadcasted_iota(jnp.int32, (N, N), 1)
    for s in range(2):
        re, im = obj[s, 0], obj[s, 1]
        to_left = jnp.where(lane < HALF, re, pltpu.roll(im, HALF, 1))
        to_right = jnp.where(lane < HALF, pltpu.roll(re, HALF, 1), im)
        send_a[s] = choose(even, to_right, to_left)
        send_b[s] = choose(even, to_left, to_right)


def extend_kernel(obj, got_a, got_b, send_a, send_b):
    even_row, even = parity_of("row") == 0, parity_of("col") == 0
    lane = lax.broadcasted_iota(jnp.int32, (N, N), 1)
    for s in range(2):
        left, right = choose(even, got_b[s], got_a[s]), choose(even, got_a[s], got_b[s])
        re = jnp.where(lane < HALF, right, pltpu.roll(left, HALF, 1))
        im = jnp.where(lane < HALF, pltpu.roll(right, HALF, 1), left)
        for q, side in enumerate((re, im)):
            for t, part in enumerate((obj[s, q], side)):
                cols = slice(t * N, (t + 1) * N)
                send_a[s, q, :, cols] = choose(even_row, part[HALF:], part[:HALF])
                send_b[s, q, :, cols] = choose(even_row, part[:HALF], part[HALF:])


def main_kernel(pos, own_a, own_b, got_a, got_b, probe, wave, inten, tabs, send_a, send_b, keep_a, keep_b,
                measured, sem, pad, acc, xh, xl, zh, zl, inner, second):
    parity = parity_of("row")
    starts = (2 - parity, 1 + parity, 3 - 3 * parity, 3 * parity)
    for start, ref in zip(starts, (own_a, own_b, got_a, got_b)):
        rows = pl.ds(pl.multiple_of(start * HALF, HALF), HALF)
        for t in range(2):
            pad[:, :, t, rows, :] = ref[:, :, :, t * N:(t + 1) * N]
    fetch = pltpu.make_async_copy(inten.at[0, 0], measured, sem)
    fetch.start()
    acc[...] = jnp.zeros_like(acc)

    lane = lax.broadcasted_iota(jnp.int32, (N, N), 1)

    def window(s, q, k):
        rows = pl.ds(pos[k, 0], N)
        begin = lax.rem(pos[k, 1] + 3 * HALF, WIDE)
        tile = begin // N
        turn = lax.rem(WIDE - begin, N)
        one = pltpu.roll(pad[s, q, tile, rows, :], turn, 1)
        two = pltpu.roll(pad[s, q, 1 - tile, rows, :], turn, 1)
        return jnp.where(lane < N - lax.rem(begin, N), one, two)

    def scatter(s, q, k, value):
        rows = pl.ds(pos[k, 0], N)
        moved = pltpu.roll(value, lax.rem(pos[k, 1], N), 1)
        fits = lane >= pos[k, 1]
        acc[s, q, 0, rows, :] = acc[s, q, 0, rows, :] + jnp.where(fits, moved, 0.0)
        acc[s, q, 1, rows, :] = acc[s, q, 1, rows, :] + jnp.where(fits, 0.0, moved)

    def put(g, b, re, im):
        rows = slice(b * N, (b + 1) * N)
        for q, part in enumerate((re, im)):
            high, low = split(part)
            xh[g, rows, q * N:(q + 1) * N] = high
            xl[g, rows, q * N:(q + 1) * N] = low

    def dot(a, b):
        return jnp.dot(a, b, preferred_element_type=F32)

    def right(g, t):
        high, low = xh[g], xl[g]
        y = dot(high, tabs[2 * t]) + dot(low, tabs[2 * t]) + dot(high, tabs[2 * t + 1])
        for b in range(2):
            for q in range(2):
                h, l = split(y[b * N:(b + 1) * N, q * N:(q + 1) * N])
                zh[g, q * N:(q + 1) * N, b * N:(b + 1) * N] = h
                zl[g, q * N:(q + 1) * N, b * N:(b + 1) * N] = l

    def left(g, t):
        high, low = zh[g], zl[g]
        y = dot(tabs[2 * t], high) + dot(tabs[2 * t], low) + dot(tabs[2 * t + 1], high)
        return [(y[:N, b * N:(b + 1) * N], y[N:, b * N:(b + 1) * N]) for b in range(2)]

    groups = range(3)
    for g in groups:
        for b in range(2):
            k = 2 * g + b
            re, im = times(probe[0], probe[1], window(0, 0, k), window(0, 1, k))
            put(g, b, re, im)
    for g in groups:
        right(g, 0)
    for g in groups:
        for b, (re, im) in enumerate(left(g, 1)):
            put(g, b, *times(wave[0], wave[1], re, im))
    for g in groups:
        right(g, 1)
    for g in groups:
        for b, (re, im) in enumerate(left(g, 0)):
            k = 2 * g + b
            inner[k, 0], inner[k, 1] = re, im
            o_re, o_im = window(1, 0, k), window(1, 1, k)
            second[k, 0], second[k, 1] = o_re, o_im
            put(g, b, *times(re, im, o_re, o_im))
    for g in groups:
        right(g, 0)
    fetch.wait()
    for g in groups:
        for b, (re, im) in enumerate(left(g, 1)):
            misfit = re * re + im * im - measured[2 * g + b]
            put(g, b, misfit * re, misfit * im)
    for g in groups:
        right(g, 1)
    for g in groups:
        for b, (re, im) in enumerate(left(g, 0)):
            k = 2 * g + b
            put(g, b, *times_conj(second[k, 0], second[k, 1], re, im))
            for q, part in enumerate(times_conj(inner[k, 0], inner[k, 1], re, im)):
                scatter(1, q, k, part)
    for g in groups:
        right(g, 0)
    for g in groups:
        for b, (re, im) in enumerate(left(g, 1)):
            put(g, b, *times_conj(wave[0], wave[1], re, im))
    for g in groups:
        right(g, 1)
    for g in groups:
        for b, (re, im) in enumerate(left(g, 0)):
            k = 2 * g + b
            for q, part in enumerate(times_conj(probe[0], probe[1], re, im)):
                scatter(0, q, k, part)
    for t in range(2):
        cols = slice(t * N, (t + 1) * N)
        for start, ref in zip(starts, (keep_a, keep_b, send_a, send_b)):
            rows = pl.ds(pl.multiple_of(start * HALF, HALF), HALF)
            ref[..., cols] = acc[:, :, t, rows, :]


def wave_kernel(phase, wave):
    wave[0] = jnp.cos(phase[...])
    wave[1] = jnp.sin(phase[...])


def fold_kernel(keep, got, send_a, send_b):
    even = parity_of("col") == 0
    total = keep[...] + got[...]
    left, right = total[..., :N], total[..., N:]
    send_a[...] = choose(even, right, left)
    send_b[...] = choose(even, left, right)


def update_kernel(own, sent_a, sent_b, got_a, got_b, out):
    even = parity_of("col") == 0
    for s in range(2):
        for q in range(2):
            one, two = sent_a[s, q] + got_a[s, q], sent_b[s, q] + got_b[s, q]
            values = pltpu.roll(own[s, q], HALF, 1)
            out[s, q, :, :N] = values[:, :N] - STEP * choose(even, two, one)
            out[s, q, :, N:] = values[:, N:] - STEP * choose(even, one, two)


HBM = pl.BlockSpec(memory_space=pltpu.HBM)
VM = pl.BlockSpec(memory_space=pltpu.VMEM)
SM = pl.BlockSpec(memory_space=pltpu.SMEM)


def shape(*dims):
    return jax.ShapeDtypeStruct(dims, F32)


def call(kernel, outs, args, scratch=(), smem=0, limit=6, anys=(), cost=1 << 20):
    specs = [SM] * smem + [VM] * (len(args) - smem)
    for k in anys:
        specs[k] = HBM
    return pl.pallas_call(
        kernel,
        out_shape=outs,
        in_specs=specs,
        out_specs=[VM] * len(outs),
        scratch_shapes=list(scratch),
        cost_estimate=pl.CostEstimate(flops=cost, bytes_accessed=cost, transcendentals=0),
        compiler_params=pltpu.CompilerParams(vmem_limit_bytes=limit << 20),
    )(*args)


def place_kernel(starts, *refs):
    value_a, value_b, out, sems = refs[0], refs[1], refs[-2], refs[-1]
    parity = parity_of("row")
    copies = []
    for k, (value, (even, odd)) in enumerate(zip((value_a, value_b), starts)):
        rows = pl.ds(pl.multiple_of((even + (odd - even) * parity) * HALF, HALF), HALF)
        copies.append(pltpu.make_async_copy(value, out.at[:, :, rows, :], sems.at[k]))
    for copy in copies:
        copy.start()
    for copy in copies:
        copy.wait()


def put_rows(value_a, value_b, starts, out=None):
    args = [value_a, value_b] + ([] if out is None else [out])
    return pl.pallas_call(
        functools.partial(place_kernel, starts),
        out_shape=shape(2, 2, WIDE, WIDE),
        in_specs=[VM, VM] + [HBM] * (len(args) - 2),
        out_specs=HBM,
        scratch_shapes=[pltpu.SemaphoreType.DMA((2,))],
        input_output_aliases={} if out is None else {2: 0},
        cost_estimate=pl.CostEstimate(flops=1 << 20, bytes_accessed=1 << 20, transcendentals=0),
        compiler_params=pltpu.CompilerParams(vmem_limit_bytes=2 << 20),
    )(*args)


def swap(value_a, value_b, axis):
    count = lax.axis_size(axis)

    def pairs(first):
        found = [(i, i + 1) for i in range(first, count - 1, 2)]
        return found + [(target, source) for source, target in found]

    got_b = lax.ppermute(value_b, axis, pairs(1))
    got_a = lax.ppermute(value_a, axis, pairs(0))
    return got_a, got_b


def per_device(obj, positions, probe, phase, intensity):
    strip, half = shape(2, 2, HALF, WIDE), shape(2, 2, HALF, N)
    side_a, side_b = call(pack_kernel, [shape(2, N, N)] * 2, [obj])
    side_a, side_b = swap(side_a, side_b, "col")
    wave, = call(wave_kernel, [shape(2, N, N)], [phase])
    own_a, own_b = call(extend_kernel, [strip] * 2, [obj, side_a, side_b])
    far_a, far_b = swap(own_a, own_b, "row")
    scratch = [
        pltpu.VMEM((6, N, N), F32), pltpu.SemaphoreType.DMA,
        pltpu.VMEM((2, 2, 2, WIDE, N), F32), pltpu.VMEM((2, 2, 2, WIDE, N), F32),
        pltpu.VMEM((3, WIDE, WIDE), BF), pltpu.VMEM((3, WIDE, WIDE), BF),
        pltpu.VMEM((3, WIDE, WIDE), BF), pltpu.VMEM((3, WIDE, WIDE), BF),
        pltpu.VMEM((6, 2, N, N), F32), pltpu.VMEM((6, 2, N, N), F32),
    ]
    g_a, g_b, keep_a, keep_b = call(
        main_kernel, [strip] * 4,
        [positions[0, 0], own_a, own_b, far_a, far_b, probe, wave,
         pltpu.with_memory_space_constraint(intensity, pltpu.HBM), jnp.asarray(tables())],
        scratch, smem=1, limit=24, anys=(7,), cost=1 << 26)
    g_a, g_b = swap(g_a, g_b, "row")

    def finish(own, keep, got):
        sent_a, sent_b = call(fold_kernel, [half] * 2, [keep, got])
        got_a, got_b = swap(sent_a, sent_b, "col")
        return call(update_kernel, [strip], [own, sent_a, sent_b, got_a, got_b])[0]

    new_b = finish(own_b, keep_b, g_b)
    new_a = finish(own_a, keep_a, g_a)
    out_a, out_b = swap(new_a, new_b, "row")
    out = put_rows(new_a, new_b, ((2, 1), (1, 2)))
    return put_rows(out_a, out_b, ((3, 0), (0, 3)), out)


def solution(mesh):
    return jax.shard_map(
        per_device,
        mesh=mesh,
        in_specs=(
            P(None, None, "row", "col"),
            P("row", "col", None, None),
            P(),
            P(),
            P("row", "col", None, None, None),
        ),
        out_specs=P(None, None, "row", "col"),
        check_vma=False,
    )
```

```python
import functools

import jax
import jax.numpy as jnp
import numpy as np
from jax import lax
from jax.experimental import pallas as pl
from jax.experimental.pallas import tpu as pltpu
from jax.sharding import PartitionSpec as P

N = 128
HALF = 64
WIDE = 256
STEP = 2.0
BF = jnp.bfloat16
F32 = jnp.float32


def tables():
    counter = np.arange(N)
    angles = 2.0 * np.pi / N * (counter[:, None] * counter[None, :] % N)
    cos, sin = np.cos(angles), np.sin(angles)
    first = np.block([[cos, -sin], [sin, cos]]) / N
    second = np.block([[cos, sin], [-sin, cos]])
    out = []
    for table in (first, second):
        table = table.astype(np.float32)
        high = table.astype(BF)
        low = (table - high.astype(np.float32)).astype(BF)
        out += [high, low]
    return np.stack(out)


def split(value):
    high = value.astype(BF)
    return high, (value - high.astype(F32)).astype(BF)


def times(ar, ai, br, bi):
    return ar * br - ai * bi, ar * bi + ai * br


def times_conj(ar, ai, br, bi):
    return ar * br + ai * bi, ar * bi - ai * br


def parity_of(axis):
    return lax.rem(lax.axis_index(axis), 2)


def choose(flag, one, two):
    return jnp.where(flag, one, two)


def pack(centre, send_a, send_b):
    even = parity_of("col") == 0
    lane = lax.broadcasted_iota(jnp.int32, send_a.shape[1:], 1)
    for s in range(2):
        re, im = centre[s, 0], centre[s, 1]
        to_left = jnp.where(lane < HALF, re, pltpu.roll(im, HALF, 1))
        to_right = jnp.where(lane < HALF, pltpu.roll(re, HALF, 1), im)
        send_a[s] = choose(even, to_right, to_left)
        send_b[s] = choose(even, to_left, to_right)


def sides(s, got_a, got_b):
    even = parity_of("col") == 0
    lane = lax.broadcasted_iota(jnp.int32, got_a.shape[1:], 1)
    left, right = choose(even, got_b[s], got_a[s]), choose(even, got_a[s], got_b[s])
    re = jnp.where(lane < HALF, right, pltpu.roll(left, HALF, 1))
    im = jnp.where(lane < HALF, pltpu.roll(right, HALF, 1), left)
    return re, im


def begin_kernel(obj, far, send_a, send_b):
    even_row = parity_of("row") == 0
    far[...] = choose(even_row, obj[:, :, :HALF, :], obj[:, :, HALF:, :])
    pack(obj, send_a, send_b)


def extend_kernel(obj, got_a, got_b, own_a, own_b):
    even_row = parity_of("row") == 0
    for s in range(2):
        for q, side in enumerate(sides(s, got_a, got_b)):
            for t, part in enumerate((obj[s, q], side)):
                cols = slice(t * N, (t + 1) * N)
                own_a[s, q, :, cols] = choose(even_row, part[HALF:], part[:HALF])
                own_b[s, q, :, cols] = choose(even_row, part[:HALF], part[HALF:])


def corner_kernel(centre, got_a, got_b, far):
    for s in range(2):
        for q, side in enumerate(sides(s, got_a, got_b)):
            far[s, q, :, :N] = centre[s, q]
            far[s, q, :, N:] = side


def main_kernel(pos, own_a, own_b, got_a, got_b, probe, phase, inten, tabs, send_a, keep_a, block,
                measured, sem, pad, acc, hre, him, xh, xl, zh, zl, inner, second):
    parity = parity_of("row")
    starts = (2 - parity, 1 + parity, 3 - 3 * parity, 3 * parity)
    for start, ref in zip(starts, (own_a, own_b, got_a, got_b)):
        rows = pl.ds(pl.multiple_of(start * HALF, HALF), HALF)
        for t in range(2):
            pad[:, :, t, rows, :] = ref[:, :, :, t * N:(t + 1) * N]
    fetch = pltpu.make_async_copy(inten.at[0, 0], measured, sem)
    fetch.start()
    acc[...] = jnp.zeros_like(acc)
    hre[...] = jnp.cos(phase[...])
    him[...] = jnp.sin(phase[...])

    lane = lax.broadcasted_iota(jnp.int32, (N, N), 1)

    def window(s, q, k):
        rows = pl.ds(pos[k, 0], N)
        begin = lax.rem(pos[k, 1] + 3 * HALF, WIDE)
        tile = begin // N
        turn = lax.rem(WIDE - begin, N)
        one = pltpu.roll(pad[s, q, tile, rows, :], turn, 1)
        two = pltpu.roll(pad[s, q, 1 - tile, rows, :], turn, 1)
        return jnp.where(lane < N - lax.rem(begin, N), one, two)

    def scatter(s, q, k, value):
        rows = pl.ds(pos[k, 0], N)
        moved = pltpu.roll(value, lax.rem(pos[k, 1], N), 1)
        fits = lane >= pos[k, 1]
        acc[s, q, 0, rows, :] = acc[s, q, 0, rows, :] + jnp.where(fits, moved, 0.0)
        acc[s, q, 1, rows, :] = acc[s, q, 1, rows, :] + jnp.where(fits, 0.0, moved)

    def put(g, b, re, im):
        rows = slice(b * N, (b + 1) * N)
        for q, part in enumerate((re, im)):
            high, low = split(part)
            xh[g, rows, q * N:(q + 1) * N] = high
            xl[g, rows, q * N:(q + 1) * N] = low

    def dot(a, b):
        return jnp.dot(a, b, preferred_element_type=F32)

    def right(g, t):
        high, low = xh[g], xl[g]
        y = dot(high, tabs[2 * t]) + dot(low, tabs[2 * t]) + dot(high, tabs[2 * t + 1])
        for b in range(2):
            for q in range(2):
                h, l = split(y[b * N:(b + 1) * N, q * N:(q + 1) * N])
                zh[g, q * N:(q + 1) * N, b * N:(b + 1) * N] = h
                zl[g, q * N:(q + 1) * N, b * N:(b + 1) * N] = l

    def left(g, t):
        high, low = zh[g], zl[g]
        y = dot(tabs[2 * t], high) + dot(tabs[2 * t], low) + dot(tabs[2 * t + 1], high)
        return [(y[:N, b * N:(b + 1) * N], y[N:, b * N:(b + 1) * N]) for b in range(2)]

    groups = range(3)
    for g in groups:
        for b in range(2):
            k = 2 * g + b
            re, im = times(probe[0], probe[1], window(0, 0, k), window(0, 1, k))
            put(g, b, re, im)
    for g in groups:
        right(g, 0)
    for g in groups:
        for b, (re, im) in enumerate(left(g, 1)):
            put(g, b, *times(hre[...], him[...], re, im))
    for g in groups:
        right(g, 1)
    for g in groups:
        for b, (re, im) in enumerate(left(g, 0)):
            k = 2 * g + b
            inner[k, 0], inner[k, 1] = re, im
            o_re, o_im = window(1, 0, k), window(1, 1, k)
            second[k, 0], second[k, 1] = o_re, o_im
            put(g, b, *times(re, im, o_re, o_im))
    for g in groups:
        right(g, 0)
    fetch.wait()
    for g in groups:
        for b, (re, im) in enumerate(left(g, 1)):
            misfit = re * re + im * im - measured[2 * g + b]
            put(g, b, misfit * re, misfit * im)
    for g in groups:
        right(g, 1)
    for g in groups:
        for b, (re, im) in enumerate(left(g, 0)):
            k = 2 * g + b
            put(g, b, *times_conj(second[k, 0], second[k, 1], re, im))
            for q, part in enumerate(times_conj(inner[k, 0], inner[k, 1], re, im)):
                scatter(1, q, k, part)
    for g in groups:
        right(g, 0)
    for g in groups:
        for b, (re, im) in enumerate(left(g, 1)):
            put(g, b, *times_conj(hre[...], him[...], re, im))
    for g in groups:
        right(g, 1)
    for g in groups:
        for b, (re, im) in enumerate(left(g, 0)):
            k = 2 * g + b
            for q, part in enumerate(times_conj(probe[0], probe[1], re, im)):
                scatter(0, q, k, part)
    for t in range(2):
        cols = slice(t * N, (t + 1) * N)
        for start, ref, height in ((starts[2], send_a, HALF), (starts[0], keep_a, HALF), (2 * parity, block, N)):
            rows = pl.ds(pl.multiple_of(start * HALF, HALF), height)
            ref[..., cols] = acc[:, :, t, rows, :]


def fold_kernel(block, got_b, keep_a, got_a, send_a, send_b):
    even = parity_of("col") == 0
    for rows, one, two in ((slice(0, N), block, got_b), (slice(N, N + HALF), keep_a, got_a)):
        total = one[...] + two[...]
        left, right = total[..., :N], total[..., N:]
        send_a[:, :, rows, :] = choose(even, right, left)
        send_b[:, :, rows, :] = choose(even, left, right)


def update_kernel(own_a, own_b, far, sent_a, sent_b, got_a, got_b, new_a, new_b):
    even_row, even = parity_of("row") == 0, parity_of("col") == 0
    for s in range(2):
        for q in range(2):
            one, two = sent_a[s, q] + got_a[s, q], sent_b[s, q] + got_b[s, q]
            total = [choose(even, two, one), choose(even, one, two)]
            first, last = far[s, q], own_b[s, q]
            parts = (choose(even_row, first, last), choose(even_row, last, first), own_a[s, q])
            for k, part in enumerate(parts):
                values = pltpu.roll(part, HALF, 1)
                rows = slice(k * HALF, (k + 1) * HALF)
                for t in range(2):
                    cols = slice(t * N, (t + 1) * N)
                    out = values[:, cols] - STEP * total[t][rows]
                    if k == 2:
                        new_a[s, q, :, cols] = out
                    else:
                        new_b[s, q, rows, cols] = out


HBM = pl.BlockSpec(memory_space=pltpu.HBM)
VM = pl.BlockSpec(memory_space=pltpu.VMEM)
SM = pl.BlockSpec(memory_space=pltpu.SMEM)


def shape(*dims):
    return jax.ShapeDtypeStruct(dims, F32)


def call(kernel, outs, args, scratch=(), smem=0, limit=6, anys=(), cost=1 << 20):
    specs = [SM] * smem + [VM] * (len(args) - smem)
    for k in anys:
        specs[k] = HBM
    return pl.pallas_call(
        kernel,
        out_shape=outs,
        in_specs=specs,
        out_specs=[VM] * len(outs),
        scratch_shapes=list(scratch),
        cost_estimate=pl.CostEstimate(flops=cost, bytes_accessed=cost, transcendentals=0),
        compiler_params=pltpu.CompilerParams(vmem_limit_bytes=limit << 20),
    )(*args)


def place_kernel(starts, *refs):
    out, sems = refs[-2], refs[-1]
    parity = parity_of("row")
    copies = []
    for k, (even, odd) in enumerate(starts):
        value = refs[k]
        rows = pl.ds(pl.multiple_of((even + (odd - even) * parity) * HALF, HALF), value.shape[2])
        copies.append(pltpu.make_async_copy(value, out.at[:, :, rows, :], sems.at[k]))
    for copy in copies:
        copy.start()
    for copy in copies:
        copy.wait()


def put_rows(values, starts, out=None):
    args = list(values) + ([] if out is None else [out])
    return pl.pallas_call(
        functools.partial(place_kernel, starts),
        out_shape=shape(2, 2, WIDE, WIDE),
        in_specs=[VM] * len(values) + [HBM] * (len(args) - len(values)),
        out_specs=HBM,
        scratch_shapes=[pltpu.SemaphoreType.DMA((len(values),))],
        input_output_aliases={} if out is None else {len(values): 0},
        cost_estimate=pl.CostEstimate(flops=1 << 20, bytes_accessed=1 << 20, transcendentals=0),
        compiler_params=pltpu.CompilerParams(vmem_limit_bytes=2 << 20),
    )(*args)


def swap(value, axis, first):
    found = [(i, i + 1) for i in range(first, lax.axis_size(axis) - 1, 2)]
    return lax.ppermute(value, axis, found + [(target, source) for source, target in found])


def per_device(obj, positions, probe, phase, intensity):
    strip, half = shape(2, 2, HALF, WIDE), shape(2, 2, N + HALF, N)
    far, side_a, side_b = call(begin_kernel, [shape(2, 2, HALF, N)] + [shape(2, N, N)] * 2, [obj])
    far = swap(far, "row", 1)
    side_b = swap(side_b, "col", 1)
    side_a = swap(side_a, "col", 0)
    corner_a, corner_b = call(pack, [shape(2, HALF, N)] * 2, [far])
    corner_b = swap(corner_b, "col", 1)
    corner_a = swap(corner_a, "col", 0)
    own_a, own_b = call(extend_kernel, [strip] * 2, [obj, side_a, side_b])
    far_a = swap(own_a, "row", 0)
    far_b, = call(corner_kernel, [strip], [far, corner_a, corner_b])
    scratch = [
        pltpu.VMEM((6, N, N), F32), pltpu.SemaphoreType.DMA,
        pltpu.VMEM((2, 2, 2, WIDE, N), F32), pltpu.VMEM((2, 2, 2, WIDE, N), F32),
        pltpu.VMEM((N, N), F32), pltpu.VMEM((N, N), F32),
        pltpu.VMEM((3, WIDE, WIDE), BF), pltpu.VMEM((3, WIDE, WIDE), BF),
        pltpu.VMEM((3, WIDE, WIDE), BF), pltpu.VMEM((3, WIDE, WIDE), BF),
        pltpu.VMEM((6, 2, N, N), F32), pltpu.VMEM((6, 2, N, N), F32),
    ]
    g_a, keep_a, block = call(
        main_kernel, [strip] * 2 + [shape(2, 2, N, WIDE)],
        [positions[0, 0], own_a, own_b, far_a, far_b, probe, phase,
         pltpu.with_memory_space_constraint(intensity, pltpu.HBM), jnp.asarray(tables())],
        scratch, smem=1, limit=24, anys=(7,), cost=1 << 26)
    got_b = swap(block, "row", 1)
    got_a = swap(g_a, "row", 0)
    half_a, half_b = call(fold_kernel, [half] * 2, [block, got_b, keep_a, got_a])
    h_b = swap(half_b, "col", 1)
    h_a = swap(half_a, "col", 0)
    new_a, new_b = call(
        update_kernel, [strip, shape(2, 2, N, WIDE)], [own_a, own_b, far_b, half_a, half_b, h_a, h_b], limit=8)
    out_a = swap(new_a, "row", 0)
    out = put_rows((new_b, new_a), ((0, 2), (2, 1)))
    return put_rows((out_a,), ((3, 0),), out)


def solution(mesh):
    return jax.shard_map(
        per_device,
        mesh=mesh,
        in_specs=(
            P(None, None, "row", "col"),
            P("row", "col", None, None),
            P(),
            P(),
            P("row", "col", None, None, None),
        ),
        out_specs=P(None, None, "row", "col"),
        check_vma=False,
    )
```
